32 devices in a mesh: lon: 16 (over z, y, core), ch: 2 (over x).
Axes of the slice: x: 2, y: 2, z: 4, core: 2. Of those that a mesh axis runs over, the one named last changes fastest.
Arguments:
- features: bfloat16 [512, 1, 8, 2048], P('ch', None, None, 'lon'), may hold values from -160 to 160, as said below
- group_norm_gain: float32 [512], P('ch'), may hold values from 0.5 to 2
- group_norm_bias: float32 [512], P('ch'), may hold values from -1 to 1
- kernel: bfloat16 [3, 3, 512, 512], P(None, None, 'ch'), may hold values from -0.058925565 to 0.058925565, as said below
- cotangent: bfloat16 [512, 1, 8, 2048], P('ch', None, None, 'lon'), may hold values from -10 to 10, as said below
Outputs:
- conv_out: bfloat16 [512, 1, 8, 2048], P('ch', None, None, 'lon')
- feature_map_gradient: bfloat16 [512, 1, 8, 2048], P('ch', None, None, 'lon')
- kernel_grad: float32 [3, 3, 512, 512], P(None, None, 'ch')
The draws below stay inside these ranges and needn't reach their ends.
Inputs may be any that keep to these rules, and one draw needn't show every extreme that they name: `features`: Real-valued feature map whose magnitude varies between rows and between longitudes, with a per-channel offset. `kernel`: Real-valued weights of standard deviation about (4608)^(-1/2). `cotangent`: Real-valued output gradient.
All inputs are finite; a program needn't handle non-finite values.
Results may differ from the reference program's by a relative error of at most 0.005.
Values may be sent and summed in bfloat16 or wider, within the bound.
No kernel may reach another device: no remote copies, remote signals or barrier semaphores. Data moves between devices by JAX's collectives and lax.ppermute only.
A program may use at most 64 MiB of HBM per device.

```python
import math
import jax
import jax.numpy as jnp
from jax import lax

C = 512
O = 512
G = 32
F = 1
H = 8
W = 2048


def feature_parts(key):
    keys = jax.random.split(jax.random.fold_in(key, 7), 4)
    along = jnp.arange(W, dtype=jnp.float32) / W
    col_scale = jnp.exp(math.log(3.0) * along + jax.random.uniform(keys[0], (W,), jnp.float32, 0.0, math.log(3.4)))
    row_scale = jnp.exp(jax.random.uniform(keys[1], (H,), jnp.float32, 0.0, math.log(3.0)))
    offsets = 0.5 * jax.random.normal(keys[2], (C,), jnp.float32)
    base = jnp.clip(jax.random.normal(keys[3], (C, F, H, W), jnp.float32), -4.0, 4.0)
    field = base * row_scale[None, None, :, None] * col_scale[None, None, None, :] + offsets[:, None, None, None]
    return (base, field)


def shared_kernel(key):
    raw = jax.random.normal(jax.random.fold_in(key, 13), (3, 3, C, O), jnp.float32)
    return jnp.clip(raw, -4.0, 4.0) * (9.0 * C) ** (-0.5)


def draw_features(key, part):
    base, field = feature_parts(key)
    return field.astype(jnp.bfloat16)


def draw_kernel(key, part):
    return shared_kernel(key).astype(jnp.bfloat16)


def draw_cotangent(key, part):
    keys = jax.random.split(jax.random.fold_in(key, 11), 2)
    base, field = feature_parts(key)
    center = shared_kernel(key)[1, 1].astype(jnp.bfloat16).astype(jnp.float32)
    mixed = jnp.einsum('co,cfhw->ofhw', center, base, precision=lax.Precision.HIGHEST)
    noise = jnp.clip(jax.random.normal(keys[0], (O, F, H, W), jnp.float32), -4.0, 4.0)
    strength = 2.0
    offsets = 0.05 * jax.random.normal(keys[1], (O,), jnp.float32)
    values = jnp.clip(strength * mixed + noise + offsets[:, None, None, None], -10.0, 10.0)
    return values.astype(jnp.bfloat16)


def shard_levels(stream_key, shape, pieces, smallest, high):
    level, own = 1.0, jax.random.fold_in(stream_key, 6)
    for position, parts in pieces:
        steps = jnp.exp(jax.random.uniform(jax.random.fold_in(own, position), (parts,), jnp.float32, smallest / len(pieces), high / len(pieces)))
        level = level * jnp.repeat(steps, shape[position] // parts).reshape([-1 if axis == position else 1 for axis in range(len(shape))])
    return level


def setup_inputs(seed: int = 0) -> dict:
    streams_of = jax.random.split(jax.random.key(seed), 6)
    features = draw_features(jax.random.fold_in(streams_of[5], 71), 0)
    group_norm_gain = jnp.clip(jnp.exp(math.log(2.0) - 1.3862944 * jax.random.uniform(streams_of[1], (C,), jnp.float32) ** shard_levels(streams_of[1], (C,), ((0, 2),), -0.2, 0.2)), 0.5, 2.0)
    group_norm_bias = jnp.clip(jax.random.uniform(streams_of[2], (C,), jnp.float32, -1.0, 1.0) * shard_levels(streams_of[2], (C,), ((0, 2),), -0.4, 0.0), -1.0, 1.0)
    kernel = draw_kernel(jax.random.fold_in(streams_of[5], 71), 0)
    cotangent = draw_cotangent(jax.random.fold_in(streams_of[5], 71), 0)
    return dict(features=features, group_norm_gain=group_norm_gain, group_norm_bias=group_norm_bias, kernel=kernel, cotangent=cotangent)


def shifted(field, row_off, col_off):
    height = field.shape[2]
    padded = jnp.pad(field, ((0, 0), (0, 0), (1, 1), (0, 0)))
    rows = padded[:, :, row_off:row_off + height, :]
    return jnp.roll(rows, 1 - col_off, axis=3)

def group_totals(field):
    return field.reshape(G, -1).sum(axis=1)

def channel_values(values):
    return jnp.repeat(values, C // G)[:, None, None, None]

def reference(features, group_norm_gain, group_norm_bias, kernel, cotangent):
    feature_map = features.astype(jnp.float32)
    element_count = float(C // G * F * H * W)
    group_mean = group_totals(feature_map) / element_count
    var = group_totals(feature_map * feature_map) / element_count - group_mean * group_mean
    inverse_deviation = 1.0 / jnp.sqrt(var + 1e-06)
    normalized_input = (feature_map - channel_values(group_mean)) * channel_values(inverse_deviation)
    preactivation = normalized_input * group_norm_gain[:, None, None, None] + group_norm_bias[:, None, None, None]
    sig = jax.nn.sigmoid(preactivation)
    act = (preactivation * sig).astype(jnp.bfloat16)
    act_f = act.astype(jnp.float32)
    kern_f = kernel.astype(jnp.float32)
    grad_f = cotangent.astype(jnp.float32)
    conv_out = jnp.zeros((O, F, H, W), jnp.float32)
    act_grad = jnp.zeros((C, F, H, W), jnp.float32)
    grad_rows = []
    for row_off in range(3):
        grad_cols = []
        for col_off in range(3):
            moved = shifted(act_f, row_off, col_off)
            conv_out = conv_out + jnp.einsum('co,cfhw->ofhw', kern_f[row_off, col_off], moved)
            grad_cols.append(jnp.einsum('cfhw,ofhw->co', moved, grad_f))
            back = shifted(grad_f, 2 - row_off, 2 - col_off)
            act_grad = act_grad + jnp.einsum('co,ofhw->cfhw', kern_f[row_off, col_off], back)
        grad_rows.append(jnp.stack(grad_cols))
    kernel_grad = jnp.stack(grad_rows) * float(F * H * W) ** (-0.5)
    preactivation_gradient = act_grad * sig * (1.0 + preactivation * (1.0 - sig))
    normalized_input_gradient = preactivation_gradient * group_norm_gain[:, None, None, None]
    linear_sum = group_totals(normalized_input_gradient)
    quadratic_sum = group_totals(normalized_input_gradient * normalized_input)
    feature_map_gradient = channel_values(inverse_deviation) * (normalized_input_gradient - channel_values(linear_sum) / element_count - normalized_input * channel_values(quadratic_sum) / element_count)
    return (conv_out.astype(jnp.bfloat16), feature_map_gradient.astype(jnp.bfloat16), kernel_grad)
```

```python
import jax
import jax.numpy as jnp
from jax import lax
from jax.sharding import PartitionSpec as P

C = 512
G = 32


def factors(count):
    half = count // 2
    rows = 1
    while (rows * 2) ** 2 <= half:
        rows *= 2
    return rows, half // rows


def shift_pairs(count, stride, size, step):
    pairs = []
    for i in range(count):
        digit = (i // stride) % size
        pairs.append((i, i + ((digit + step) % size - digit) * stride))
    return pairs


class Ring:
    def __init__(self, axis, stride, size):
        self.axis, self.stride, self.size = axis, stride, size
        self.count = lax.axis_size(axis)
        self.digit = (lax.axis_index(axis) // stride) % size

    def send(self, value, step):
        return lax.ppermute(value, self.axis, shift_pairs(self.count, self.stride, self.size, step))

    def scatter(self, values, dim):
        def piece(step):
            return lax.dynamic_index_in_dim(
                values, (self.digit + step) % self.size, dim, keepdims=False
            )

        total = piece(0)
        for step in range(1, self.size):
            total = total + self.send(piece(step).astype(jnp.bfloat16), step).astype(jnp.float32)
        return total

    def gather(self, value, dim):
        parts = [value] + [self.send(value, self.size - step) for step in range(1, self.size)]
        ordered = []
        for place in range(self.size):
            which = (place - self.digit) % self.size
            if self.size == 2:
                ordered.append(jnp.where(which == 0, parts[0], parts[1]))
            else:
                ordered.append(lax.select_n(which, *parts))
        return jnp.stack(ordered, axis=dim)


def butterfly(value, axis):
    count = lax.axis_size(axis)
    mask = 1
    while mask < count:
        value = value + lax.ppermute(value, axis, [(i, i ^ mask) for i in range(count)])
        mask *= 2
    return value


def edge_columns(block):
    count = lax.axis_size("lon")
    forward = [(i, (i + 1) % count) for i in range(count)]
    backward = [(j, i) for i, j in forward]
    low = lax.ppermute(block[..., -1], "lon", forward)
    high = lax.ppermute(block[..., 0], "lon", backward)
    return low, high


def pad_rows(field):
    return jnp.pad(field, ((0, 0), (1, 1), (0, 0)))


def group_sums(field, size):
    return field.reshape(field.shape[0] // size, -1).sum(axis=1)


def kernel_grad_sum(block):
    taps, chans, outs = block.shape
    count = lax.axis_size("lon")
    rows, cols = factors(count)
    core, row, col = Ring("lon", 1, 2), Ring("lon", 2, rows), Ring("lon", 2 * rows, cols)
    block = block.reshape(taps, 2, rows, cols, chans // count, outs)
    block = core.scatter(block, 1)
    first, second = block[:6], block[6:]
    second = col.scatter(second, 2)
    first = row.scatter(first, 1)
    first = col.scatter(first, 1)
    second = row.scatter(second, 1)
    first = first.astype(jnp.bfloat16)
    second = second.astype(jnp.bfloat16)
    first = col.gather(first, 1)
    second = row.gather(second, 1)
    first = row.gather(first, 1)
    second = col.gather(second, 2)
    block = jnp.concatenate([first, second], axis=0)
    block = core.gather(block, 1)
    return block.reshape(taps, chans, outs).astype(jnp.float32)


def per_device(features, group_norm_gain, group_norm_bias, kernel, cotangent):
    size = C // G
    chans, frames, height, width = features.shape
    out_local = cotangent.shape[0]
    strips = lax.axis_size("lon")
    sides = Ring("ch", 1, lax.axis_size("ch"))
    count = float(size * frames * height * width * strips)
    features = features.reshape(chans, height, width)
    cotangent = cotangent.reshape(out_local, height, width)
    feature_map = features.astype(jnp.float32)
    sums = jnp.stack([group_sums(feature_map, size), group_sums(feature_map * feature_map, size)])
    sums = butterfly(sums, "lon")
    group_mean = sums[0] / count
    var = sums[1] / count - group_mean * group_mean
    inverse = 1.0 / jnp.sqrt(var + 1e-06)
    mean_c = jnp.repeat(group_mean, size)[:, None, None]
    inverse_c = jnp.repeat(inverse, size)[:, None, None]
    gain_c = group_norm_gain[:, None, None]
    bias_c = group_norm_bias[:, None, None]

    low, high = edge_columns(jnp.concatenate([features, cotangent], axis=0))
    rim = jnp.stack([low[:chans], high[:chans]], axis=2).astype(jnp.float32)

    def normal(value):
        return (value - mean_c) * inverse_c

    normalized = normal(feature_map)
    pre = normalized * gain_c + bias_c
    sig = jax.nn.sigmoid(pre)
    act = (pre * sig).astype(jnp.bfloat16)
    pre_rim = normal(rim) * gain_c + bias_c
    act_rim = (pre_rim * jax.nn.sigmoid(pre_rim)).astype(jnp.bfloat16)
    act_pad = pad_rows(jnp.concatenate([act_rim[:, :, :1], act, act_rim[:, :, 1:]], axis=2))

    body = sides.gather(cotangent, 0).reshape(-1, height, width)
    grad_rim = sides.gather(jnp.stack([low[chans:], high[chans:]], axis=2), 0)
    grad_rim = grad_rim.reshape(-1, height, 2)
    grad_pad = pad_rows(jnp.concatenate([grad_rim[:, :, :1], body, grad_rim[:, :, 1:]], axis=2))

    total = jnp.zeros((body.shape[0], height, width), jnp.float32)
    act_grad = jnp.zeros((chans, height, width), jnp.float32)
    taps = []
    for r in range(3):
        for s in range(3):
            patch = act_pad[:, r : r + height, s : s + width]
            taps.append(jnp.einsum("chw,ohw->co", patch, body, preferred_element_type=jnp.float32))
    kernel_grad = kernel_grad_sum(jnp.stack(taps))
    kernel_grad = kernel_grad * float(frames * height * width * strips) ** (-0.5)
    for r in range(3):
        for s in range(3):
            patch = act_pad[:, r : r + height, s : s + width]
            total = total + jnp.einsum(
                "co,chw->ohw", kernel[r, s], patch, preferred_element_type=jnp.float32
            )
            back = grad_pad[:, 2 - r : 2 - r + height, 2 - s : 2 - s + width]
            act_grad = act_grad + jnp.einsum(
                "co,ohw->chw", kernel[r, s], back, preferred_element_type=jnp.float32
            )
    conv_out = sides.scatter(total.reshape(sides.size, out_local, height, width), 0)

    pre_grad = act_grad * sig * (1.0 + pre * (1.0 - sig))
    grad_hat = pre_grad * gain_c
    sums = jnp.stack([group_sums(grad_hat, size), group_sums(grad_hat * normalized, size)])
    sums = butterfly(sums, "lon")
    linear_c = jnp.repeat(sums[0], size)[:, None, None]
    quadratic_c = jnp.repeat(sums[1], size)[:, None, None]
    gradient = inverse_c * (grad_hat - linear_c / count - normalized * quadratic_c / count)
    shape = (chans, frames, height, width)
    return (
        conv_out.astype(jnp.bfloat16).reshape(out_local, frames, height, width),
        gradient.astype(jnp.bfloat16).reshape(shape),
        kernel_grad.reshape(3, 3, chans, -1),
    )


def solution(mesh):
    in_specs = (
        P("ch", None, None, "lon"),
        P("ch"),
        P("ch"),
        P(None, None, "ch", None),
        P("ch", None, None, "lon"),
    )
    out_specs = (P("ch", None, None, "lon"), P("ch", None, None, "lon"), P(None, None, "ch", None))
    return jax.shard_map(
        per_device, mesh=mesh, in_specs=in_specs, out_specs=out_specs, check_vma=False
    )
```

```python
import functools
import jax
import jax.numpy as jnp
from jax import lax
from jax.experimental import pallas as pl
from jax.experimental.pallas import tpu as pltpu
from jax.sharding import PartitionSpec as P

C = 512
G = 32
EPS = 1e-06
F32 = jnp.float32
BF16 = jnp.bfloat16
LANES = 128
NN = (((1,), (0,)), ((), ()))
NT = (((1,), (1,)), ((), ()))
TN = (((0,), (0,)), ((), ()))


def factors(count):
    half = count // 2
    rows = 1
    while (rows * 2) ** 2 <= half:
        rows *= 2
    return rows, half // rows


def shift_pairs(count, stride, size, step):
    pairs = []
    for i in range(count):
        digit = (i // stride) % size
        pairs.append((i, i + ((digit + step) % size - digit) * stride))
    return pairs


class Ring:
    def __init__(self, axis, stride, size):
        self.axis, self.stride, self.size = axis, stride, size
        self.count = lax.axis_size(axis)
        self.digit = (lax.axis_index(axis) // stride) % size

    def send(self, value, step):
        pairs = shift_pairs(self.count, self.stride, self.size, step)
        return lax.ppermute(value, self.axis, pairs)

    def relative(self, step):
        return (self.digit + step) % self.size

    def scatter(self, values, dim):
        def piece(step):
            return lax.dynamic_index_in_dim(values, self.relative(step), dim, keepdims=False)

        total = piece(0)
        for step in range(1, self.size):
            total = total + self.send(piece(step).astype(BF16), step).astype(F32)
        return total

    def parts(self, value):
        sends = [self.send(value, self.size - step) for step in range(1, self.size)]
        return [value] + sends

    def gather(self, value, dim):
        parts = self.parts(value)
        ordered = []
        for place in range(self.size):
            which = (place - self.digit) % self.size
            if self.size == 2:
                ordered.append(jnp.where(which == 0, parts[0], parts[1]))
            else:
                ordered.append(lax.select_n(which, *parts))
        return jnp.stack(ordered, axis=dim)


def butterfly(value, axis):
    count = lax.axis_size(axis)
    step = 0
    while (1 << step) < count:
        pairs = [(i, i ^ (1 << step)) for i in range(count)]
        value = value + lax.ppermute(value, axis, pairs)
        step += 1
    return value


def dot(a, b, dims):
    return lax.dot_general(a, b, dims, preferred_element_type=F32)


def grouped(field, size):
    return field.reshape(field.shape[0] // size, size, field.shape[1]).sum(axis=1)


def stats_kernel(size, feature_ref, sums_ref):
    value = feature_ref[...].astype(F32)
    groups = sums_ref.shape[0] // 2
    sums_ref[:groups] = grouped(value, size)
    sums_ref[groups:] = grouped(value * value, size)


def flatten(height, source, target, edge_ref, wide):
    width = source.shape[1]
    chans, cells = target.shape
    row = lax.broadcasted_iota(jnp.int32, (cells, LANES), 0)
    col = lax.broadcasted_iota(jnp.int32, (cells, LANES), 1)
    first = (col < height) & (row == col * width)
    last = (col >= height) & (col < 2 * height) & (row == (col - height) * width + width - 1)
    pick = jnp.where(first | last, 1.0, 0.0).astype(BF16)
    wide[...] = source[...].astype(F32)
    for h in range(height):
        target[:, h * width : (h + 1) * width] = wide[pl.ds(h, chans, stride=height), :].astype(
            BF16
        )
    edge_ref[...] = dot(target[...], pick, NN).astype(BF16)


def prep_cot_kernel(height, place_ref, source, target, edge_ref, wide):
    flatten(height, source, target, edge_ref, wide)


def prep_feature_kernel(
    height, source, gain_ref, bias_ref, target, edge_ref, gain_out, bias_out, wide
):
    flatten(height, source, target, edge_ref, wide)
    chans = target.shape[0]
    row = lax.broadcasted_iota(jnp.int32, (chans, chans), 0)
    col = lax.broadcasted_iota(jnp.int32, (chans, chans), 1)
    for vector, out in ((gain_ref, gain_out), (bias_ref, bias_out)):
        column = jnp.sum(jnp.where(row == col, vector[...], 0.0), axis=1, keepdims=True)
        out[...] = jnp.broadcast_to(column, (chans, LANES))


def channel_stats(sums, count, size):
    totals = jnp.sum(sums, axis=1, keepdims=True)
    groups = totals.shape[0] // 2
    mean = totals[:groups] / count
    var = totals[groups:] / count - mean * mean
    inverse = 1.0 / jnp.sqrt(var + EPS)
    return spread(mean, size), spread(inverse, size)


def spread(values, size):
    groups = values.shape[0]
    wide = jnp.broadcast_to(values[:, :, None], (groups, size, LANES))
    return wide.reshape(groups * size, LANES)


def fill_shifted(target, rows, base, height, width, tile, low, high):
    lane = lax.broadcasted_iota(jnp.int32, (rows, width), 1)
    blank = jnp.zeros((rows, width), BF16)
    for s in range(3):
        band = slice(base + s * rows, base + (s + 1) * rows)
        target[band, :width] = blank
        target[band, (height + 1) * width :] = blank
    for h in range(height):
        value = tile(h)
        left = jnp.where(lane == 0, low[:, height + h : height + h + 1], pltpu.roll(value, 1, 1))
        right = jnp.where(lane == width - 1, high[:, h : h + 1], pltpu.roll(value, width - 1, 1))
        place = slice((h + 1) * width, (h + 2) * width)
        for s, shifted in enumerate((left, value, right)):
            target[base + s * rows : base + (s + 1) * rows, place] = shifted.astype(BF16)


def silu(pre):
    return pre * jax.nn.sigmoid(pre)


def preactivation(value, stats):
    mean, inverse, gain, bias = stats
    normal = (value.astype(F32) - mean) * inverse
    return normal, normal * gain + bias


def fill_active(target, base, height, width, flat, low, high, stats):
    rows = flat.shape[0]

    def tile(h):
        return silu(preactivation(flat[:, h * width : (h + 1) * width], stats)[1])

    low_act = silu(preactivation(low[...], stats)[1])
    high_act = silu(preactivation(high[...], stats)[1])
    fill_shifted(target, rows, base, height, width, tile, low_act, high_act)


def wgrad_kernel(
    count, size, parts, rows, cols, height, width, place_ref, flat_a, flat_b, low_a, high_a, low_b,
    high_b, sums_ref, gain_ref, bias_ref, *rest
):
    cots = rest[: 2 * parts]
    outs_refs = rest[2 * parts : -8]
    act, cot, mean_buf, inverse_buf, flats, edges, vectors, sem = rest[-8:]
    chans, cells = flat_a.shape
    half = chans // 2
    piece = half // (rows * cols)
    outs = cot.shape[1] // parts
    exact = piece % 16 == 0
    step = pl.program_id(0)

    def copies():
        for k in range(2):
            for j in range(parts):
                start = pl.multiple_of(place_ref[2 + j] * outs, outs)
                yield pltpu.make_async_copy(
                    cots[k * parts + j], cot.at[k, pl.ds(start, outs)], sem.at[k, j]
                )

    @pl.when(step == 0)
    def _():
        for copy in copies():
            copy.start()
        mean, inverse = channel_stats(sums_ref[...], count, size)
        mean_buf[...] = mean
        inverse_buf[...] = inverse
        moves = [(place_ref[0] * half, 0, half)]
        if exact:
            moves = []
            for y in range(rows):
                for z in range(cols):
                    source = place_ref[0] * half
                    source += place_ref[2 + parts + y] * (cols * piece)
                    source += place_ref[2 + parts + rows + z] * piece
                    moves.append((source, (y * cols + z) * piece, piece))
        for source, target, amount in moves:
            here = pl.ds(pl.multiple_of(source, amount), amount)
            there = slice(target, target + amount)
            for k, ref in enumerate((flat_a, flat_b)):
                flats[k, there] = ref[here, :]
            for k, ref in enumerate((low_a, high_a, low_b, high_b)):
                edges[k, there] = ref[here, :]
            for k, ref in enumerate((mean_buf, inverse_buf, gain_ref, bias_ref)):
                vectors[k, there] = ref[here, :]
        stats = tuple(vectors[k] for k in range(4))
        for k in range(2):
            fill_active(
                act.at[k], 0, height, width, flats.at[k], edges.at[2 * k], edges.at[2 * k + 1],
                stats,
            )
        for copy in copies():
            copy.wait()

    offset = pl.multiple_of(step * width, width)
    total = dot(act[0, :, pl.ds(offset, cells)], cot[0], NT)
    total = total + dot(act[1, :, pl.ds(offset, cells)], cot[1], NT)
    if not exact:
        outs_refs[0][0] = total.reshape(3, half, total.shape[1])
        return
    total = total.reshape(3, rows, cols, piece, total.shape[1])

    @pl.when(step < 2)
    def _():
        for y in range(rows):
            outs_refs[y][...] = total[:, y].astype(outs_refs[y].dtype)

    @pl.when(step == 2)
    def _():
        for z in range(cols):
            outs_refs[rows + z][...] = total[:, :, z].astype(outs_refs[rows + z].dtype)


def conv_kernel(
    count, size, parts, height, width, place_ref, flat, low, high, sums_ref, gain_ref, bias_ref,
    kernel_ref, keep_ref, *rest
):
    sends = rest[: parts - 1]
    act, total = rest[parts - 1 :]
    cells = height * width
    outs = keep_ref.shape[0]
    mean, inverse = channel_stats(sums_ref[...], count, size)
    stats = (mean, inverse, gain_ref[...], bias_ref[...])
    fill_active(act, 0, height, width, flat, low, high, stats)
    for r in range(3):
        piece = dot(kernel_ref[r], act[:, r * width : r * width + cells], TN)
        if r:
            total[...] += piece
        else:
            total[...] = piece
    for j in range(parts):
        start = pl.multiple_of(place_ref[2 + j] * outs, outs)
        value = total[pl.ds(start, outs), :]
        if j:
            sends[j - 1][...] = value.astype(BF16)
        else:
            keep_ref[...] = value


def agrad_kernel(
    count, size, parts, height, width, place_ref, flat, sums_ref, gain_ref, bias_ref, kernel_ref,
    *rest
):
    cots, lows, highs = rest[:parts], rest[parts : 2 * parts], rest[2 * parts : 3 * parts]
    grad_ref, partial_ref, cot = rest[3 * parts :]
    cells = height * width
    outs = cots[0].shape[0]
    chans = flat.shape[0]
    for j in range(parts):
        start = pl.multiple_of(place_ref[2 + j] * outs, outs)
        source, low, high = cots[j], lows[j][...].astype(F32), highs[j][...].astype(F32)
        lane = lax.broadcasted_iota(jnp.int32, (outs, width), 1)
        blank = jnp.zeros((outs, width), BF16)
        for s in range(3):
            cot[s, pl.ds(start, outs), :width] = blank
            cot[s, pl.ds(start, outs), (height + 1) * width :] = blank
        for h in range(height):
            value = source[:, h * width : (h + 1) * width].astype(F32)
            left = jnp.where(
                lane == 0, low[:, height + h : height + h + 1], pltpu.roll(value, 1, 1)
            )
            right = jnp.where(
                lane == width - 1, high[:, h : h + 1], pltpu.roll(value, width - 1, 1)
            )
            for s, shifted in enumerate((left, value, right)):
                cot[s, pl.ds(start, outs), (h + 1) * width : (h + 2) * width] = shifted.astype(BF16)
    total = jnp.zeros((chans, cells), F32)
    for r in range(3):
        for s in range(3):
            total = total + dot(
                kernel_ref[r, s * chans : (s + 1) * chans],
                cot[2 - s, :, (2 - r) * width : (2 - r) * width + cells],
                NN,
            )
    grad_ref[...] = total
    mean, inverse = channel_stats(sums_ref[...], count, size)
    stats = (mean, inverse, gain_ref[...], bias_ref[...])
    linear = jnp.zeros((chans, width), F32)
    quadratic = jnp.zeros((chans, width), F32)
    for h in range(height):
        place = slice(h * width, (h + 1) * width)
        normal, pre = preactivation(flat[:, place], stats)
        sig = jax.nn.sigmoid(pre)
        grad = grad_ref[:, place] * sig * (1.0 + pre * (1.0 - sig)) * stats[2]
        grad_ref[:, place] = grad
        linear = linear + grad
        quadratic = quadratic + grad * normal
    groups = partial_ref.shape[0] // 2
    partial_ref[:groups] = grouped(linear, size)
    partial_ref[groups:] = grouped(quadratic, size)


def gradient_kernel(
    count, size, height, width, flat, grad_ref, sums_ref, partial_ref, out_ref, wide
):
    chans = flat.shape[0]
    mean, inverse = channel_stats(sums_ref[...], count, size)
    totals = jnp.sum(partial_ref[...], axis=1, keepdims=True) / count
    groups = totals.shape[0] // 2
    linear, quadratic = spread(totals[:groups], size), spread(totals[groups:], size)
    for h in range(height):
        place = slice(h * width, (h + 1) * width)
        normal = (flat[:, place].astype(F32) - mean) * inverse
        value = inverse * (grad_ref[:, place] - linear - normal * quadratic)
        wide[pl.ds(h, chans, stride=height), :] = value
    out_ref[...] = wide[...].astype(BF16)


def convout_kernel(height, width, keep_ref, *rest):
    received, (out_ref, wide) = rest[:-2], rest[-2:]
    outs = keep_ref.shape[0]
    for h in range(height):
        place = slice(h * width, (h + 1) * width)
        value = keep_ref[:, place]
        for other in received:
            value = value + other[:, place].astype(F32)
        wide[pl.ds(h, outs, stride=height), :] = value
    out_ref[...] = wide[...].astype(BF16)


def generic_sum(block):
    taps, half, outs = block.shape
    count = lax.axis_size("lon")
    rows, cols = factors(count)
    row, col = Ring("lon", 2, rows), Ring("lon", 2 * rows, cols)
    block = block.reshape(taps, rows, cols, half // (rows * cols), outs)
    first, second = block[:6], block[6:]
    second = col.scatter(second, 2)
    first = row.scatter(first, 1)
    first = col.scatter(first, 1)
    second = row.scatter(second, 1)
    first = first.astype(BF16)
    second = second.astype(BF16)
    first = col.gather(first, 1)
    second = row.gather(second, 1)
    first = row.gather(first, 1)
    second = col.gather(second, 2)
    return jnp.concatenate([first, second], axis=0).reshape(taps, half, outs)


def generic_assemble(scale, place_ref, own_ref, other_ref, out_ref):
    half = own_ref.shape[1]
    mine = pl.multiple_of(place_ref[0] * half, half)
    theirs = pl.multiple_of(place_ref[1] * half, half)
    out_ref[0, pl.ds(mine, half), :] = own_ref[0].astype(F32) * scale
    out_ref[0, pl.ds(theirs, half), :] = other_ref[0].astype(F32) * scale


def assemble_kernel(scale, parts, rows, cols, order, first, place_ref, *rest):
    out_ref, buffer, sem = rest[-3:]
    sources = rest[: len(order)]
    taps, piece = buffer.shape[1], buffer.shape[2]
    copies = []
    for source, (core, blocks) in zip(sources, order):
        for i, (y, z) in enumerate(blocks):
            n = len(copies)
            buffer[n] = source[i].astype(F32) * scale
            start = place_ref[core] * (rows * cols * piece)
            start += place_ref[2 + parts + y] * (cols * piece)
            start += place_ref[2 + parts + rows + z] * piece
            start = pl.multiple_of(start, piece)
            copy = pltpu.make_async_copy(
                buffer.at[n], out_ref.at[pl.ds(first, taps), pl.ds(start, piece)], sem.at[n]
            )
            copy.start()
            copies.append(copy)
    for copy in copies:
        copy.wait()


def per_device(features, group_norm_gain, group_norm_bias, kernel, cotangent):
    size = C // G
    chans, frames, height, width = features.shape
    out_local = cotangent.shape[0]
    strips = lax.axis_size("lon")
    parts = lax.axis_size("ch")
    rows, cols = factors(strips)
    outs = parts * out_local
    cells = height * width
    half = chans // 2
    piece = half // (rows * cols)
    exact = piece % 16 == 0
    groups = chans // size
    count = float(size * frames * height * width * strips)
    scale = float(frames * height * width * strips) ** (-0.5)
    core, side = Ring("lon", 1, 2), Ring("ch", 1, parts)
    row, col = Ring("lon", 2, rows), Ring("lon", 2 * rows, cols)
    shape = jax.ShapeDtypeStruct
    vmem = pl.BlockSpec(memory_space=pltpu.VMEM)
    smem = pl.BlockSpec(memory_space=pltpu.SMEM)
    anywhere = pl.BlockSpec(memory_space=pl.ANY)

    def call(body, **options):
        def run(*operands):
            return pl.pallas_call(body, **options)(*operands)

        return run

    feature_rows = features.reshape(chans * height, width)
    cot_rows = cotangent.reshape(out_local * height, width)
    weights = kernel.reshape(3, 3 * chans, outs)
    places = [core.digit, 1 - core.digit]
    places += [side.relative(j) for j in range(parts)]
    places += [row.relative(j) for j in range(rows)]
    places += [col.relative(j) for j in range(cols)]
    place = jnp.stack(places).astype(jnp.int32)

    sums = call(
        functools.partial(stats_kernel, size * height), out_shape=shape((2 * groups, width), F32)
    )(feature_rows)
    sums = butterfly(sums, "lon")

    cot, cot_edges = call(
        functools.partial(prep_cot_kernel, height),
        out_shape=(shape((out_local, cells), BF16), shape((out_local, LANES), BF16)),
        in_specs=[smem, vmem],
        scratch_shapes=[pltpu.VMEM((out_local * height, width), F32)],
    )(place, cot_rows)
    flat, edges, gain, bias = call(
        functools.partial(prep_feature_kernel, height),
        out_shape=(
            shape((chans, cells), BF16),
            shape((chans, LANES), BF16),
            shape((chans, LANES), F32),
            shape((chans, LANES), F32),
        ),
        scratch_shapes=[pltpu.VMEM((chans * height, width), F32)],
    )(feature_rows, group_norm_gain[None, :], group_norm_bias[None, :])

    cots = side.parts(cot)
    forward = [(i, (i + 1) % strips) for i in range(strips)]
    backward = [(j, i) for i, j in forward]
    low = lax.ppermute(edges, "lon", forward)
    high = lax.ppermute(edges, "lon", backward)
    lows = side.parts(lax.ppermute(cot_edges, "lon", forward))
    highs = side.parts(lax.ppermute(cot_edges, "lon", backward))
    other_flat = core.send(flat, 1)
    other_low = core.send(low, 1)
    other_high = core.send(high, 1)
    other_cots = [core.send(value, 1) for value in cots]

    if exact:
        widths = [(3, cols, piece, outs)] * rows + [(3, rows, piece, outs)] * cols
        kinds = [F32] + [BF16] * (rows - 1) + [F32] + [BF16] * (cols - 1)
        out_shape = [
            shape((6,) + dims[1:] if i < rows else dims, kind)
            for i, (dims, kind) in enumerate(zip(widths, kinds))
        ]
        out_specs = [
            pl.BlockSpec(dims, (lambda r: (jnp.minimum(r, 1), 0, 0, 0)))
            if i < rows
            else pl.BlockSpec(dims, lambda r: (0, 0, 0, 0))
            for i, dims in enumerate(widths)
        ]
    else:
        out_shape = [shape((3, 3, half, outs), F32)]
        out_specs = [pl.BlockSpec((1, 3, half, outs), lambda r: (r, 0, 0, 0))]
    blocks = call(
        functools.partial(wgrad_kernel, count, size, parts, rows, cols, height, width),
        out_shape=out_shape,
        grid=(3,),
        in_specs=[smem] + [vmem] * 9 + [anywhere] * (2 * parts),
        out_specs=out_specs,
        scratch_shapes=[
            pltpu.VMEM((2, 3 * half, cells + 2 * width), BF16),
            pltpu.VMEM((2, outs, cells), BF16),
            pltpu.VMEM((chans, LANES), F32),
            pltpu.VMEM((chans, LANES), F32),
            pltpu.VMEM((2, half, cells), BF16),
            pltpu.VMEM((4, half, LANES), BF16),
            pltpu.VMEM((4, half, LANES), F32),
            pltpu.SemaphoreType.DMA((2, parts)),
        ],
    )(
        place, flat, other_flat, low, high, other_low, other_high, sums, gain, bias, *cots,
        *other_cots
    )
    if exact:
        first, second = blocks[0], blocks[rows]
        for y in range(1, rows):
            first = first + row.send(blocks[y], y).astype(F32)
        for z in range(1, cols):
            second = second + col.send(blocks[rows + z], z).astype(F32)
        total = first[:, 0]
        for z in range(1, cols):
            total = total + col.send(first[:, z].astype(BF16), z).astype(F32)
        first = total.astype(BF16)
        total = second[:, 0]
        for y in range(1, rows):
            total = total + row.send(second[:, y].astype(BF16), y).astype(F32)
        second = total.astype(BF16)
        first = jnp.stack(col.parts(first))
        firsts = row.parts(first)
        second = jnp.stack(row.parts(second))
        seconds = jnp.concatenate(col.parts(second), axis=0)
        other_seconds = core.send(seconds, 1)
        other_firsts = [core.send(value, 1) for value in firsts]
        second_blocks = [(y, z) for z in range(cols) for y in range(rows)]
        order = [(0, second_blocks), (1, second_blocks)]

        def assemble(order, taps, start, operands, alias):
            slots = sum(len(listed) for _, listed in order)
            return call(
                functools.partial(assemble_kernel, scale, parts, rows, cols, order, start),
                out_shape=shape((9, chans, outs), F32),
                in_specs=[smem] + [vmem] * len(order) + [anywhere] * len(alias),
                out_specs=anywhere,
                scratch_shapes=[
                    pltpu.VMEM((slots, taps, piece, outs), F32),
                    pltpu.SemaphoreType.DMA((slots,)),
                ],
                input_output_aliases={1 + len(order): 0} if alias else {},
            )(place, *operands, *alias)

        kernel_grad = assemble(order, 3, 6, [seconds, other_seconds], [])
        order = [(c, [(y, z) for z in range(cols)]) for c in range(2) for y in range(rows)]
        kernel_grad = assemble(order, 6, 0, firsts + other_firsts, [kernel_grad])
    else:
        own = generic_sum(blocks[0].reshape(9, half, outs))
        kernel_grad = call(
            functools.partial(generic_assemble, scale),
            out_shape=shape((9, chans, outs), F32),
            grid=(9,),
            in_specs=[smem] + [pl.BlockSpec((1, half, outs), lambda t: (t, 0, 0))] * 2,
            out_specs=pl.BlockSpec((1, chans, outs), lambda t: (t, 0, 0)),
        )(place, own, core.send(own, 1))

    keep, *sends = call(
        functools.partial(conv_kernel, count, size, parts, height, width),
        out_shape=[shape((out_local, cells), F32)]
        + [shape((out_local, cells), BF16)] * (parts - 1),
        in_specs=[smem] + [vmem] * 7,
        scratch_shapes=[
            pltpu.VMEM((3 * chans, cells + 2 * width), BF16),
            pltpu.VMEM((outs, cells), F32),
        ],
    )(place, flat, low, high, sums, gain, bias, weights)
    received = [side.send(value, j + 1) for j, value in enumerate(sends)]
    conv_out = call(
        functools.partial(convout_kernel, height, width),
        out_shape=shape((out_local * height, width), BF16),
        scratch_shapes=[pltpu.VMEM((out_local * height, width), F32)],
    )(keep, *received)

    grad_hat, partial = call(
        functools.partial(agrad_kernel, count, size, parts, height, width),
        out_shape=(shape((chans, cells), F32), shape((2 * groups, width), F32)),
        in_specs=[smem] + [vmem] * (5 + 3 * parts),
        scratch_shapes=[pltpu.VMEM((3, outs, cells + 2 * width), BF16)],
    )(place, flat, sums, gain, bias, weights, *cots, *lows, *highs)
    partial = butterfly(partial, "lon")
    gradient = call(
        functools.partial(gradient_kernel, count, size, height, width),
        out_shape=shape((chans * height, width), BF16),
        scratch_shapes=[pltpu.VMEM((chans * height, width), F32)],
    )(flat, grad_hat, sums, partial)
    return (
        conv_out.reshape(cotangent.shape),
        gradient.reshape(features.shape),
        kernel_grad.reshape(3, 3, chans, outs),
    )


def solution(mesh):
    in_specs = (
        P("ch", None, None, "lon"),
        P("ch"),
        P("ch"),
        P(None, None, "ch", None),
        P("ch", None, None, "lon"),
    )
    out_specs = (P("ch", None, None, "lon"), P("ch", None, None, "lon"), P(None, None, "ch", None))

    return jax.shard_map(
        per_device, mesh=mesh, in_specs=in_specs, out_specs=out_specs, check_vma=False
    )
```
